32 devices in a mesh: seq: 8 (over y, x, core), chan: 4 (over z).
Axes of the slice: x: 2, y: 2, z: 4, core: 2. Of those that a mesh axis runs over, the one named last changes fastest.
Arguments:
- hidden_states: bfloat16 [4096, 2048], P('chan', 'seq'), may hold values from -700 to 700
- norm_gain: float32 [4096], P('chan'), may hold values from 0.1 to 1.9
- short_filter: float32 [4096, 128], P('chan'), may hold values from -0.5 to 0.5
- long_filter: bfloat16 [4096, 2048], P('chan', 'seq'), may hold values from -0.125 to 0.125
- long_bias: float32 [4096], P('chan'), may hold values from -4 to 4
- gate_stream: bfloat16 [4096, 2048], P('chan', 'seq'), may hold values from -6 to 6
- upstream: bfloat16 [4096, 2048], P(None, 'seq'), may hold values from -6 to 6
Outputs:
- mixed: bfloat16 [4096, 2048], P('chan', 'seq')
- weight_grad: float32 [4096, 4096], P('seq', 'chan')
The draws below stay inside these ranges and needn't reach their ends.
All inputs are finite; a program needn't handle non-finite values.
Results may differ from the reference program's by a relative error of at most 0.015.
Values may be sent and summed in bfloat16 or wider, within the bound.
A program may use at most 64 MiB of HBM per device.

```python
import math
import jax
import jax.numpy as jnp
from jax import lax

D = 4096
TAPS = 128
SEQ = 2048


def draw_hidden_states(key, part):
    key_chan, key_tok, key_base = jax.random.split(jax.random.fold_in(key, 11), 3)
    channel = jnp.arange(D, dtype=jnp.float32)
    chan_scale = 3.0 ** (0.5 * channel / D) * jnp.exp(jax.random.uniform(key_chan, (D,), jnp.float32, 0.0, math.log(10.0)))
    tok_scale = jnp.exp(jax.random.uniform(key_tok, (SEQ,), jnp.float32, 0.0, math.log(10.0)))
    base = jax.random.truncated_normal(key_base, -4.0, 4.0, (D, SEQ), jnp.float32)
    return (base * chan_scale[:, None] * tok_scale[None, :]).astype(jnp.bfloat16)


def spiked(array, key, source, target, parts, factor):
    def block_of(dim):
        return (jnp.arange(array.shape[dim]) // (array.shape[dim] // parts)).reshape((-1,) + (1,) * (array.ndim - 1 - dim))

    one_side = jax.random.permutation(key, parts)[block_of(target)]
    second = (block_of(target) + parts // 2) % parts
    return jnp.where((block_of(source) == one_side) | (block_of(source) == second), factor * array, array)


def block_scale(stream_key, dims, cuts, low, largest):
    factor_of = 1.0
    for dim, parts in cuts:
        draws = jax.random.uniform(jax.random.fold_in(jax.random.fold_in(stream_key, 6), dim), (parts,), jnp.float32, low / len(cuts), largest / len(cuts))
        factor_of = factor_of * jnp.repeat(jnp.exp(draws), dims[dim] // parts).reshape((-1,) + (1,) * (len(dims) - 1 - dim))
    return factor_of


def noise(own_key, extent, deviation, limit, shards=(), kind=jnp.bfloat16):
    factor_of = block_scale(own_key, extent, shards, -0.22, 0.18) if shards else 1.0
    drawn = jax.random.normal(own_key, extent, jnp.float32) * deviation * factor_of
    return jnp.minimum(jnp.maximum(drawn, -limit), limit).astype(kind)


def noise_with(own_key, dims, scale, reach, pieces, heavy, kind=jnp.bfloat16):
    result = scale * jax.random.normal(own_key, dims, jnp.float32)
    if pieces:
        result = result * block_scale(own_key, dims, pieces, -0.22, 0.18)
    return jnp.clip(spiked(result, jax.random.fold_in(own_key, 3), *heavy), -reach, reach).astype(kind)


def setup_inputs(seed: int = 0) -> dict:
    keys = jax.random.split(jax.random.key(seed), 8)
    hidden_states = draw_hidden_states(jax.random.fold_in(keys[7], 71), 0)
    norm_gain = jnp.clip(1.0 + 0.18 * jax.random.normal(keys[1], (D,), jnp.float32), 0.1, 1.9)
    short_filter = noise(keys[2], (D, TAPS), TAPS ** -0.5, 0.5, ((0, 4),), jnp.float32)
    long_filter = noise(keys[3], (D, SEQ), SEQ ** -0.5, 0.125, ((0, 4), (1, 8)))
    long_bias = noise(keys[4], (D,), 1.0, 4.0, ((0, 4),), jnp.float32)
    gate_stream = noise(keys[5], (D, SEQ), 1.0, 6.0, ((0, 4), (1, 8)))
    upstream = noise_with(keys[6], (D, SEQ), 1.0, 6.0, ((1, 8),), (1, 0, 8, 2.0))
    return {"hidden_states": hidden_states, "norm_gain": norm_gain, "short_filter": short_filter, "long_filter": long_filter, "long_bias": long_bias, "gate_stream": gate_stream, "upstream": upstream}


EPSILON = 1e-05

def short_conv(padded, taps):
    seq_total = padded.shape[1] - TAPS + 1

    def add_tap(index, total):
        start = (TAPS - 1 - index).astype(jnp.int32)
        window = lax.dynamic_slice_in_dim(padded, start, seq_total, 1)
        weight = lax.dynamic_slice_in_dim(taps, index.astype(jnp.int32), 1, 1)
        return total + weight * window
    initial = jnp.zeros((padded.shape[0], seq_total), jnp.float32)
    return lax.fori_loop(jnp.int32(0), jnp.int32(TAPS), add_tap, initial)

def reference(hidden_states, norm_gain, short_filter, long_filter, long_bias, gate_stream, upstream):
    states = hidden_states.astype(jnp.float32)
    squares = lax.optimization_barrier(jnp.sum(states * states, axis=0))
    normed = (states * lax.rsqrt(squares / D + EPSILON)[None, :] * norm_gain[:, None]).astype(jnp.bfloat16)
    padded = jnp.pad(normed.astype(jnp.float32), ((0, 0), (TAPS - 1, 0)))
    short_out = short_conv(padded, short_filter.astype(jnp.float32)).astype(jnp.bfloat16)
    block_width = math.gcd(D, 256)
    length = 2 * SEQ

    def one_block(pair):
        signal, filt = pair
        spec_signal = jnp.fft.rfft(signal.astype(jnp.float32), n=length, axis=1)
        spec_filter = jnp.fft.rfft(filt.astype(jnp.float32), n=length, axis=1)
        return jnp.fft.irfft(spec_signal * spec_filter, n=length, axis=1)[:, :SEQ].astype(jnp.float32)
    blocks = (short_out.reshape(D // block_width, block_width, SEQ), long_filter.reshape(D // block_width, block_width, SEQ))
    long_conv = lax.map(one_block, blocks).reshape(D, SEQ)
    long_out = (long_conv + long_bias[:, None] * short_out.astype(jnp.float32)).astype(jnp.bfloat16)
    mixed = (gate_stream.astype(jnp.float32) * long_out.astype(jnp.float32)).astype(jnp.bfloat16)
    weight_grad = lax.dot_general(upstream, mixed, (((1,), (1,)), ((), ())), preferred_element_type=jnp.float32)
    return (mixed, weight_grad)
```

```python
import functools

import jax
import jax.numpy as jnp
from jax import lax
from jax.experimental import pallas as pl
from jax.experimental.pallas import tpu as pltpu
from jax.sharding import PartitionSpec as P

EPSILON = 1e-05
BF16 = jnp.bfloat16
F32 = jnp.float32


def body(
    n,
    nz,
    groups,
    hidden,
    gain,
    taps,
    filt,
    bias,
    gate,
    upstream,
    out_mixed,
    out_grad,
    hidden_own,
    land_hidden,
    land_filt,
    land_gate,
    taps_own,
    sq_land,
    inv_land,
    owned,
    whole,
    xs,
    hs,
    gs,
    ms,
    local_sem,
    hid_send,
    hid_recv,
    fil_send,
    fil_recv,
    gat_send,
    gat_recv,
    up_send,
    up_recv,
    sq_send,
    sq_recv,
    inv_send,
    inv_recv,
    mix_send,
    mix_recv,
    fwd_send,
):
    me = lax.axis_index("seq")
    mz = lax.axis_index("chan")
    wide, cols = hidden.shape
    width = wide // n
    rows = upstream.shape[0] // n
    block = taps.shape[1]
    per = cols // block
    blocks = n * per
    total = wide * nz
    share = width // groups
    seq_len = n * cols

    def remote(src, dst, send, recv, peer, axis="seq"):
        return pltpu.make_async_remote_copy(
            src_ref=src,
            dst_ref=dst,
            send_sem=send,
            recv_sem=recv,
            device_id={axis: peer},
            device_id_type=pl.DeviceIdType.MESH,
        )

    local = [
        pltpu.make_async_copy(hidden, hidden_own, local_sem.at[0]),
        pltpu.make_async_copy(
            hidden.at[pl.ds(me * width, width)], land_hidden.at[me], local_sem.at[1]
        ),
        pltpu.make_async_copy(taps.at[pl.ds(me * width, width)], taps_own, local_sem.at[2]),
        pltpu.make_async_copy(filt.at[pl.ds(me * width, width)], land_filt.at[me], local_sem.at[3]),
        pltpu.make_async_copy(gate.at[pl.ds(me * width, width)], land_gate.at[me], local_sem.at[4]),
        pltpu.make_async_copy(
            upstream.at[pl.ds(me * rows, rows)],
            owned.at[:, pl.ds(pl.multiple_of(me * cols, 128), cols)],
            local_sem.at[5],
        ),
    ]
    for copy in local:
        copy.start()

    barrier = pltpu.get_barrier_semaphore()
    for r in range(1, n):
        pl.semaphore_signal(
            barrier,
            inc=1,
            device_id={"seq": (me + r) % n},
            device_id_type=pl.DeviceIdType.MESH,
        )
    for r in range(1, nz):
        pl.semaphore_signal(
            barrier,
            inc=1,
            device_id={"chan": (mz + r) % nz},
            device_id_type=pl.DeviceIdType.MESH,
        )
    pl.semaphore_wait(barrier, n + nz - 2)

    sends = []

    def spread(source, land, send, recv):
        for r in range(1, n):
            peer = (me + r) % n
            copy = remote(
                source.at[pl.ds(peer * width, width)], land.at[me], send.at[r], recv.at[me], peer
            )
            copy.start()
            sends.append(copy)

    spread(hidden, land_hidden, hid_send, hid_recv)
    spread(filt, land_filt, fil_send, fil_recv)
    spread(gate, land_gate, gat_send, gat_recv)
    my_cols = pl.ds(pl.multiple_of(me * cols, 128), cols)
    for r in range(1, n):
        peer = (me + r) % n
        copy = remote(
            upstream.at[pl.ds(peer * rows, rows)],
            owned.at[:, my_cols],
            up_send.at[r],
            up_recv.at[me],
            peer,
        )
        copy.start()
        sends.append(copy)

    local[0].wait()

    def add_square(i, acc):
        part = hidden_own[pl.ds(pl.multiple_of(i * 32, 32), 32), :].astype(F32)
        part = part * part
        return acc + (part[0:8] + part[8:16]) + (part[16:24] + part[24:32])

    sq_land[mz] = lax.fori_loop(0, wide // 32, add_square, jnp.zeros((8, cols), F32), unroll=4)
    for r in range(1, nz):
        peer = (mz + r) % nz
        copy = remote(
            sq_land.at[mz], sq_land.at[mz], sq_send.at[r], sq_recv.at[mz], peer, "chan"
        )
        copy.start()
        sends.append(copy)
    for r in range(1, nz):
        peer = (mz + r) % nz
        remote(
            sq_land.at[mz], sq_land.at[peer], sq_send.at[r], sq_recv.at[peer], peer, "chan"
        ).wait_recv()
    squares = sq_land[0]
    for z in range(1, nz):
        squares = squares + sq_land[z]
    squares = jnp.sum(squares, axis=0, keepdims=True)
    inverse = lax.rsqrt(squares / total + EPSILON)
    inv_land[me] = jnp.broadcast_to(inverse, (8, cols))
    for r in range(1, n):
        peer = (me + r) % n
        copy = remote(inv_land.at[me], inv_land.at[me], inv_send.at[r], inv_recv.at[me], peer)
        copy.start()
        sends.append(copy)

    def arrived(land, send, recv):
        for r in range(1, n):
            peer = (me + r) % n
            remote(land.at[me], land.at[peer], send.at[r], recv.at[peer], peer).wait_recv()

    local[1].wait()
    local[2].wait()
    local[3].wait()
    local[4].wait()
    arrived(land_hidden, hid_send, hid_recv)
    arrived(inv_land, inv_send, inv_recv)
    for p in range(n):
        for k in range(per):
            lanes = slice(k * block, (k + 1) * block)
            spot = slice((p * per + k) * width, (p * per + k + 1) * width)
            xs[spot, :] = land_hidden[p, :, lanes].astype(F32) * inv_land[p, 0:1, lanes]
    arrived(land_filt, fil_send, fil_recv)
    for p in range(n):
        for k in range(per):
            lanes = slice(k * block, (k + 1) * block)
            spot = slice((p * per + k) * width, (p * per + k + 1) * width)
            hs[spot, :] = land_filt[p, :, lanes].astype(F32)
    arrived(land_gate, gat_send, gat_recv)
    for p in range(n):
        for k in range(per):
            lanes = slice(k * block, (k + 1) * block)
            spot = slice((p * per + k) * width, (p * per + k + 1) * width)
            gs[spot, :] = land_gate[p, :, lanes].astype(F32)

    lane_at = lax.broadcasted_iota(jnp.int32, (block, block), 1)
    row_at = lax.broadcasted_iota(jnp.int32, (block, block), 0)
    causal = lane_at >= row_at
    block_at = lax.broadcasted_iota(jnp.int32, (blocks, block), 0)

    def circulant(row):
        return pltpu.roll(
            jnp.broadcast_to(row, (block, block)), 0, 1, stride=1, stride_axis=0
        )

    def later(value, by):
        if by == 0:
            return value
        return jnp.where(block_at >= by, pltpu.roll(value, by, 0), 0.0)

    def channel(c, carry):
        mine = pl.ds(c, blocks, stride=width)
        x = (xs[mine, :] * gain[me * width + c]).astype(BF16)
        turned = circulant(taps_own[pl.ds(c, 1), :])
        now = jnp.where(causal, turned, 0.0).astype(BF16)
        before = jnp.where(causal, 0.0, turned).astype(BF16)
        pair = jnp.concatenate([x, later(x.astype(F32), 1).astype(BF16)], axis=1)
        short = jnp.dot(
            pair, jnp.concatenate([now, before], axis=0), preferred_element_type=F32
        )
        short = short.astype(BF16).astype(F32)
        acc = bias[me * width + c] * short
        held = jnp.zeros((block, block), F32)
        step = 2 if blocks % 2 == 0 else 1
        for d in range(0, blocks, step):
            signal, table = [], []
            for e in range(d, d + step):
                turned = circulant(hs[pl.ds(e * width + c, 1), :])
                table.append(jnp.where(causal, turned, held).astype(BF16))
                held = turned
                signal.append(later(short, e).astype(BF16))
            acc = acc + jnp.dot(
                jnp.concatenate(signal, axis=1),
                jnp.concatenate(table, axis=0),
                preferred_element_type=F32,
            )
        ms[mine, :] = gs[mine, :] * acc.astype(BF16).astype(F32)
        return carry

    other = me + 1 - 2 * (me % 2)

    def piece(src, g):
        return whole.at[src, pl.ds(g * share, share)]

    def forward(g):
        for k in range(1, n // 2):
            source = (me + 2 * k) % n
            remote(
                piece(me, g), piece(source, g), mix_send.at[g, k], mix_recv.at[g, source], source
            ).wait_recv()
            copy = remote(
                piece(source, g),
                piece(source, g),
                fwd_send.at[g, k],
                mix_recv.at[g, source],
                other,
            )
            copy.start()
            sends.append(copy)

    for g in range(groups):
        lax.fori_loop(g * share, (g + 1) * share, channel, 0)
        for b in range(blocks):
            start = b * width + g * share
            whole[me, g * share : (g + 1) * share, b * block : (b + 1) * block] = ms[
                start : start + share, :
            ].astype(BF16)
        for k in range(1, n // 2):
            peer = (me + 2 * k) % n
            copy = remote(
                piece(me, g), piece(me, g), mix_send.at[g, k], mix_recv.at[g, me], peer
            )
            copy.start()
            sends.append(copy)
        copy = remote(piece(me, g), piece(me, g), mix_send.at[g, 0], mix_recv.at[g, me], other)
        copy.start()
        sends.append(copy)
        if g > 0:
            forward(g - 1)
    forward(groups - 1)

    local[5].wait()
    for r in range(1, n):
        peer = (me + r) % n
        remote(
            upstream.at[pl.ds(0, rows)],
            owned.at[:, pl.ds(pl.multiple_of(peer * cols, 128), cols)],
            up_send.at[r],
            up_recv.at[peer],
            peer,
        ).wait_recv()

    for k in range(n // 2):
        source = (other + 2 * k) % n
        for g in range(groups):
            remote(
                piece(me, g), piece(source, g), mix_send.at[g, 0], mix_recv.at[g, source], other
            ).wait_recv()

    for p in range(n):
        out_mixed[p * width : (p + 1) * width, :] = whole[p, :, my_cols]

    sources = max(2, 128 // width)
    tile = min(rows, 128)
    for q in range(n // sources):
        right = whole[q * sources : (q + 1) * sources].reshape(sources * width, seq_len)

        def multiply(i, carry):
            at = pl.ds(pl.multiple_of(i * tile, tile), tile)
            out_grad[at, q * sources * width : (q + 1) * sources * width] = lax.dot_general(
                owned[at, :], right, (((1,), (1,)), ((), ())), preferred_element_type=F32
            )
            return carry

        lax.fori_loop(0, rows // tile, multiply, 0)

    for copy in sends:
        copy.wait_send()


def shards(hidden_states, norm_gain, short_filter, long_filter, long_bias, gate_stream, upstream):
    n = lax.axis_size("seq")
    nz = lax.axis_size("chan")
    wide, cols = hidden_states.shape
    width = wide // n
    rows = upstream.shape[0] // n
    seq_len = cols * n
    groups = max(1, width // 32)
    block = short_filter.shape[1]
    anywhere = pl.BlockSpec(memory_space=pl.ANY)
    scalars = pl.BlockSpec(memory_space=pltpu.SMEM)
    vmem = pl.BlockSpec(memory_space=pltpu.VMEM)
    dma = pltpu.SemaphoreType.DMA
    flat = (seq_len // block * width, block)
    return pl.pallas_call(
        functools.partial(body, n, nz, groups),
        out_shape=(
            jax.ShapeDtypeStruct((wide, cols), BF16),
            jax.ShapeDtypeStruct((rows, wide), F32),
        ),
        in_specs=[anywhere, scalars, anywhere, anywhere, scalars, anywhere, anywhere],
        out_specs=(vmem, vmem),
        scratch_shapes=[
            pltpu.VMEM((wide, cols), BF16),
            pltpu.VMEM((n, width, cols), BF16),
            pltpu.VMEM((n, width, cols), BF16),
            pltpu.VMEM((n, width, cols), BF16),
            pltpu.VMEM((width, block), F32),
            pltpu.VMEM((nz, 8, cols), F32),
            pltpu.VMEM((n, 8, cols), F32),
            pltpu.VMEM((rows, seq_len), BF16),
            pltpu.VMEM((n, width, seq_len), BF16),
            pltpu.VMEM(flat, F32),
            pltpu.VMEM(flat, F32),
            pltpu.VMEM(flat, F32),
            pltpu.VMEM(flat, F32),
            dma((6,)),
            dma((n,)),
            dma((n,)),
            dma((n,)),
            dma((n,)),
            dma((n,)),
            dma((n,)),
            dma((n,)),
            dma((n,)),
            dma((nz,)),
            dma((nz,)),
            dma((n,)),
            dma((n,)),
            dma((groups, n)),
            dma((groups, n)),
            dma((groups, n)),
        ],
        compiler_params=pltpu.CompilerParams(
            collective_id=0, has_side_effects=True, vmem_limit_bytes=48 * 1024 * 1024
        ),
        name="hyena",
    )(hidden_states, norm_gain, short_filter, long_filter, long_bias, gate_stream, upstream)


def solution(mesh):
    placed = (
        P("chan", "seq"),
        P("chan"),
        P("chan", None),
        P("chan", "seq"),
        P("chan"),
        P("chan", "seq"),
        P(None, "seq"),
    )
    return jax.shard_map(
        shards,
        mesh=mesh,
        in_specs=placed,
        out_specs=(P("chan", "seq"), P("seq", "chan")),
        check_vma=False,
    )
```

```python
import functools

import jax
import jax.numpy as jnp
from jax import lax
from jax.experimental import pallas as pl
from jax.experimental.pallas import tpu as pltpu
from jax.sharding import PartitionSpec as P

EPSILON = 1e-05
BF16 = jnp.bfloat16
F32 = jnp.float32


def body(
    n,
    nz,
    groups,
    hidden,
    gain,
    taps,
    filt,
    bias,
    gate,
    upstream,
    out_mixed,
    out_grad,
    hidden_own,
    land_hidden,
    land_filt,
    land_gate,
    taps_own,
    sq_land,
    inv_land,
    owned,
    whole,
    xs,
    hs,
    gs,
    ms,
    local_sem,
    hid_send,
    hid_recv,
    fil_send,
    fil_recv,
    gat_send,
    gat_recv,
    up_send,
    up_recv,
    part_send,
    part_recv,
    plane_send,
    plane_recv,
    sq_send,
    sq_recv,
    inv_send,
    inv_recv,
    mix_send,
    mix_recv,
    fwd_send,
):
    me = lax.axis_index("seq")
    mz = lax.axis_index("chan")
    wide, cols = hidden.shape
    width = wide // n
    rows = upstream.shape[0] // n
    block = taps.shape[1]
    per = cols // block
    blocks = n * per
    total = wide * nz
    share = width // groups
    part = rows * 3 // 4 // nz // 16 * 16
    half = rows - part * nz
    part_rows = pl.ds(pl.multiple_of(half + mz * part, 16), part)
    my_cols = pl.ds(pl.multiple_of(me * cols, 128), cols)
    seq_len = n * cols

    def remote(src, dst, send, recv, peer, axis="seq"):
        return pltpu.make_async_remote_copy(
            src_ref=src,
            dst_ref=dst,
            send_sem=send,
            recv_sem=recv,
            device_id={axis: peer},
            device_id_type=pl.DeviceIdType.MESH,
        )

    local = [
        pltpu.make_async_copy(hidden, hidden_own, local_sem.at[0]),
        pltpu.make_async_copy(
            hidden.at[pl.ds(me * width, width)], land_hidden.at[me], local_sem.at[1]
        ),
        pltpu.make_async_copy(taps.at[pl.ds(me * width, width)], taps_own, local_sem.at[2]),
        pltpu.make_async_copy(filt.at[pl.ds(me * width, width)], land_filt.at[me], local_sem.at[3]),
        pltpu.make_async_copy(gate.at[pl.ds(me * width, width)], land_gate.at[me], local_sem.at[4]),
        pltpu.make_async_copy(
            upstream.at[pl.ds(me * rows, half)], owned.at[0:half, my_cols], local_sem.at[5]
        ),
        pltpu.make_async_copy(
            upstream.at[pl.ds(me * rows + half + mz * part, part)],
            owned.at[part_rows, my_cols],
            local_sem.at[6],
        ),
    ]
    for copy in local:
        copy.start()

    barrier = pltpu.get_barrier_semaphore()
    for r in range(1, n):
        pl.semaphore_signal(
            barrier,
            inc=1,
            device_id={"seq": (me + r) % n},
            device_id_type=pl.DeviceIdType.MESH,
        )
    for r in range(1, nz):
        pl.semaphore_signal(
            barrier,
            inc=1,
            device_id={"chan": (mz + r) % nz},
            device_id_type=pl.DeviceIdType.MESH,
        )
    pl.semaphore_wait(barrier, n + nz - 2)

    sends = []

    def spread(source, land, send, recv):
        for r in range(1, n):
            peer = (me + r) % n
            copy = remote(
                source.at[pl.ds(peer * width, width)], land.at[me], send.at[r], recv.at[me], peer
            )
            copy.start()
            sends.append(copy)

    spread(hidden, land_hidden, hid_send, hid_recv)
    local[0].wait()

    def add_square(i, acc):
        part = hidden_own[pl.ds(pl.multiple_of(i * 32, 32), 32), :].astype(F32)
        part = part * part
        return acc + (part[0:8] + part[8:16]) + (part[16:24] + part[24:32])

    sq_land[mz] = lax.fori_loop(0, wide // 32, add_square, jnp.zeros((8, cols), F32), unroll=4)
    for r in range(1, nz):
        peer = (mz + r) % nz
        copy = remote(
            sq_land.at[mz], sq_land.at[mz], sq_send.at[r], sq_recv.at[mz], peer, "chan"
        )
        copy.start()
        sends.append(copy)
    for r in range(1, nz):
        peer = (mz + r) % nz
        remote(
            sq_land.at[mz], sq_land.at[peer], sq_send.at[r], sq_recv.at[peer], peer, "chan"
        ).wait_recv()
    squares = sq_land[0]
    for z in range(1, nz):
        squares = squares + sq_land[z]
    squares = jnp.sum(squares, axis=0, keepdims=True)
    inverse = lax.rsqrt(squares / total + EPSILON)
    inv_land[me] = jnp.broadcast_to(inverse, (8, cols))
    for r in range(1, n):
        peer = (me + r) % n
        copy = remote(inv_land.at[me], inv_land.at[me], inv_send.at[r], inv_recv.at[me], peer)
        copy.start()
        sends.append(copy)

    spread(filt, land_filt, fil_send, fil_recv)
    spread(gate, land_gate, gat_send, gat_recv)
    for r in range(1, n):
        peer = (me + r) % n
        copy = remote(
            upstream.at[pl.ds(peer * rows + half + mz * part, part)],
            owned.at[part_rows, my_cols],
            part_send.at[r],
            part_recv.at[me],
            peer,
        )
        copy.start()
        sends.append(copy)
    for r in range(1, n):
        peer = (me + r) % n
        copy = remote(
            upstream.at[pl.ds(peer * rows, half)],
            owned.at[0:half, my_cols],
            up_send.at[r],
            up_recv.at[me],
            peer,
        )
        copy.start()
        sends.append(copy)

    def arrived(land, send, recv):
        for r in range(1, n):
            peer = (me + r) % n
            remote(land.at[me], land.at[peer], send.at[r], recv.at[peer], peer).wait_recv()

    local[1].wait()
    local[2].wait()
    local[3].wait()
    local[4].wait()
    arrived(land_hidden, hid_send, hid_recv)
    arrived(inv_land, inv_send, inv_recv)
    for p in range(n):
        for k in range(per):
            lanes = slice(k * block, (k + 1) * block)
            spot = slice((p * per + k) * width, (p * per + k + 1) * width)
            xs[spot, :] = land_hidden[p, :, lanes].astype(F32) * inv_land[p, 0:1, lanes]
    arrived(land_filt, fil_send, fil_recv)
    for p in range(n):
        for k in range(per):
            lanes = slice(k * block, (k + 1) * block)
            spot = slice((p * per + k) * width, (p * per + k + 1) * width)
            hs[spot, :] = land_filt[p, :, lanes].astype(F32)
    arrived(land_gate, gat_send, gat_recv)
    for p in range(n):
        for k in range(per):
            lanes = slice(k * block, (k + 1) * block)
            spot = slice((p * per + k) * width, (p * per + k + 1) * width)
            gs[spot, :] = land_gate[p, :, lanes].astype(F32)

    lane_at = lax.broadcasted_iota(jnp.int32, (block, block), 1)
    row_at = lax.broadcasted_iota(jnp.int32, (block, block), 0)
    causal = lane_at >= row_at
    block_at = lax.broadcasted_iota(jnp.int32, (blocks, block), 0)

    def circulant(row):
        return pltpu.roll(
            jnp.broadcast_to(row, (block, block)), 0, 1, stride=1, stride_axis=0
        )

    def later(value, by):
        if by == 0:
            return value
        return jnp.where(block_at >= by, pltpu.roll(value, by, 0), 0.0)

    def channel(c, carry):
        mine = pl.ds(c, blocks, stride=width)
        x = (xs[mine, :] * gain[me * width + c]).astype(BF16)
        turned = circulant(taps_own[pl.ds(c, 1), :])
        now = jnp.where(causal, turned, 0.0).astype(BF16)
        before = jnp.where(causal, 0.0, turned).astype(BF16)
        pair = jnp.concatenate([x, later(x.astype(F32), 1).astype(BF16)], axis=1)
        short = jnp.dot(
            pair, jnp.concatenate([now, before], axis=0), preferred_element_type=F32
        )
        short = short.astype(BF16).astype(F32)
        acc = bias[me * width + c] * short
        held = jnp.zeros((block, block), F32)
        step = 2 if blocks % 2 == 0 else 1
        for d in range(0, blocks, step):
            signal, table = [], []
            for e in range(d, d + step):
                turned = circulant(hs[pl.ds(e * width + c, 1), :])
                table.append(jnp.where(causal, turned, held).astype(BF16))
                held = turned
                signal.append(later(short, e).astype(BF16))
            acc = acc + jnp.dot(
                jnp.concatenate(signal, axis=1),
                jnp.concatenate(table, axis=0),
                preferred_element_type=F32,
            )
        ms[mine, :] = gs[mine, :] * acc.astype(BF16).astype(F32)
        return carry

    other = me + 1 - 2 * (me % 2)

    def piece(src, g):
        return whole.at[src, pl.ds(g * share, share)]

    def forward(g):
        for k in range(1, n // 2):
            source = (me + 2 * k) % n
            remote(
                piece(me, g), piece(source, g), mix_send.at[g, k], mix_recv.at[g, source], source
            ).wait_recv()
            copy = remote(
                piece(source, g),
                piece(source, g),
                fwd_send.at[g, k],
                mix_recv.at[g, source],
                other,
            )
            copy.start()
            sends.append(copy)

    def share_part():
        local[6].wait()
        for r in range(1, n):
            peer = (me + r) % n
            remote(
                upstream.at[pl.ds(0, part)],
                owned.at[part_rows, pl.ds(pl.multiple_of(peer * cols, 128), cols)],
                part_send.at[r],
                part_recv.at[peer],
                peer,
            ).wait_recv()
        for r in range(1, nz):
            peer = (mz + r) % nz
            copy = remote(
                owned.at[part_rows],
                owned.at[part_rows],
                plane_send.at[r],
                plane_recv.at[mz],
                peer,
                "chan",
            )
            copy.start()
            sends.append(copy)

    for g in range(groups):
        lax.fori_loop(g * share, (g + 1) * share, channel, 0, unroll=8)
        for b in range(blocks):
            start = b * width + g * share
            whole[me, g * share : (g + 1) * share, b * block : (b + 1) * block] = ms[
                start : start + share, :
            ].astype(BF16)
        for k in range(1, n // 2):
            peer = (me + 2 * k) % n
            copy = remote(
                piece(me, g), piece(me, g), mix_send.at[g, k], mix_recv.at[g, me], peer
            )
            copy.start()
            sends.append(copy)
        copy = remote(piece(me, g), piece(me, g), mix_send.at[g, 0], mix_recv.at[g, me], other)
        copy.start()
        sends.append(copy)
        if g == 0:
            share_part()
        if g > 0:
            forward(g - 1)
    forward(groups - 1)

    local[5].wait()
    for r in range(1, n):
        peer = (me + r) % n
        remote(
            upstream.at[pl.ds(0, half)],
            owned.at[0:half, pl.ds(pl.multiple_of(peer * cols, 128), cols)],
            up_send.at[r],
            up_recv.at[peer],
            peer,
        ).wait_recv()

    for r in range(1, nz):
        peer = (mz + r) % nz
        remote(
            owned.at[part_rows],
            owned.at[pl.ds(pl.multiple_of(half + peer * part, 16), part)],
            plane_send.at[r],
            plane_recv.at[peer],
            peer,
            "chan",
        ).wait_recv()

    for k in range(n // 2):
        source = (other + 2 * k) % n
        for g in range(groups):
            remote(
                piece(me, g), piece(source, g), mix_send.at[g, 0], mix_recv.at[g, source], other
            ).wait_recv()

    for p in range(n):
        out_mixed[p * width : (p + 1) * width, :] = whole[p, :, my_cols]

    sources = max(2, 128 // width)
    tile = min(rows, 128)
    for q in range(n // sources):
        right = whole[q * sources : (q + 1) * sources].reshape(sources * width, seq_len)

        def multiply(i, carry):
            at = pl.ds(pl.multiple_of(i * tile, tile), tile)
            out_grad[at, q * sources * width : (q + 1) * sources * width] = lax.dot_general(
                owned[at, :], right, (((1,), (1,)), ((), ())), preferred_element_type=F32
            )
            return carry

        lax.fori_loop(0, rows // tile, multiply, 0)

    for copy in sends:
        copy.wait_send()


def shards(hidden_states, norm_gain, short_filter, long_filter, long_bias, gate_stream, upstream):
    n = lax.axis_size("seq")
    nz = lax.axis_size("chan")
    wide, cols = hidden_states.shape
    width = wide // n
    rows = upstream.shape[0] // n
    seq_len = cols * n
    groups = max(1, width // 32)
    block = short_filter.shape[1]
    anywhere = pl.BlockSpec(memory_space=pl.ANY)
    scalars = pl.BlockSpec(memory_space=pltpu.SMEM)
    vmem = pl.BlockSpec(memory_space=pltpu.VMEM)
    dma = pltpu.SemaphoreType.DMA
    flat = (seq_len // block * width, block)
    return pl.pallas_call(
        functools.partial(body, n, nz, groups),
        out_shape=(
            jax.ShapeDtypeStruct((wide, cols), BF16),
            jax.ShapeDtypeStruct((rows, wide), F32),
        ),
        in_specs=[anywhere, scalars, anywhere, anywhere, scalars, anywhere, anywhere],
        out_specs=(vmem, vmem),
        scratch_shapes=[
            pltpu.VMEM((wide, cols), BF16),
            pltpu.VMEM((n, width, cols), BF16),
            pltpu.VMEM((n, width, cols), BF16),
            pltpu.VMEM((n, width, cols), BF16),
            pltpu.VMEM((width, block), F32),
            pltpu.VMEM((nz, 8, cols), F32),
            pltpu.VMEM((n, 8, cols), F32),
            pltpu.VMEM((rows, seq_len), BF16),
            pltpu.VMEM((n, width, seq_len), BF16),
            pltpu.VMEM(flat, F32),
            pltpu.VMEM(flat, F32),
            pltpu.VMEM(flat, F32),
            pltpu.VMEM(flat, F32),
            dma((7,)),
            dma((n,)),
            dma((n,)),
            dma((n,)),
            dma((n,)),
            dma((n,)),
            dma((n,)),
            dma((n,)),
            dma((n,)),
            dma((n,)),
            dma((n,)),
            dma((nz,)),
            dma((nz,)),
            dma((nz,)),
            dma((nz,)),
            dma((n,)),
            dma((n,)),
            dma((groups, n)),
            dma((groups, n)),
            dma((groups, n)),
        ],
        compiler_params=pltpu.CompilerParams(
            collective_id=0, has_side_effects=True, vmem_limit_bytes=48 * 1024 * 1024
        ),
        name="hyena",
    )(hidden_states, norm_gain, short_filter, long_filter, long_bias, gate_stream, upstream)


def solution(mesh):
    placed = (
        P("chan", "seq"),
        P("chan"),
        P("chan", None),
        P("chan", "seq"),
        P("chan"),
        P("chan", "seq"),
        P(None, "seq"),
    )
    return jax.shard_map(
        shards,
        mesh=mesh,
        in_specs=placed,
        out_specs=(P("chan", "seq"), P("seq", "chan")),
        check_vma=False,
    )
```

```python
import functools

import jax
import jax.numpy as jnp
from jax import lax
from jax.experimental import pallas as pl
from jax.experimental.pallas import tpu as pltpu
from jax.sharding import PartitionSpec as P

EPSILON = 1e-05
BF16 = jnp.bfloat16
F32 = jnp.float32


def body(
    n,
    nz,
    groups,
    hidden,
    gain,
    taps,
    filt,
    bias,
    gate,
    upstream,
    out_mixed,
    out_grad,
    hidden_own,
    land_hidden,
    land_filt,
    land_gate,
    taps_own,
    sq_land,
    inv_land,
    owned,
    whole,
    xs,
    hs,
    gs,
    ms,
    local_sem,
    hid_send,
    hid_recv,
    fil_send,
    fil_recv,
    gat_send,
    gat_recv,
    up_send,
    up_recv,
    part_send,
    part_recv,
    plane_send,
    plane_recv,
    sq_send,
    sq_recv,
    inv_send,
    inv_recv,
    mix_send,
    mix_recv,
    fwd_send,
):
    me = lax.axis_index("seq")
    mz = lax.axis_index("chan")
    wide, cols = hidden.shape
    width = wide // n
    rows = upstream.shape[0] // n
    block = taps.shape[1]
    per = cols // block
    blocks = n * per
    total = wide * nz
    share = width // groups
    part = rows * 3 // 4 // nz // 16 * 16
    half = rows - part * nz
    part_rows = pl.ds(pl.multiple_of(half + mz * part, 16), part)
    my_cols = pl.ds(pl.multiple_of(me * cols, 128), cols)
    seq_len = n * cols

    def remote(src, dst, send, recv, peer, axis="seq"):
        return pltpu.make_async_remote_copy(
            src_ref=src,
            dst_ref=dst,
            send_sem=send,
            recv_sem=recv,
            device_id={axis: peer},
            device_id_type=pl.DeviceIdType.MESH,
        )

    local = [
        pltpu.make_async_copy(hidden, hidden_own, local_sem.at[0]),
        pltpu.make_async_copy(
            hidden.at[pl.ds(me * width, width)], land_hidden.at[me], local_sem.at[1]
        ),
        pltpu.make_async_copy(taps.at[pl.ds(me * width, width)], taps_own, local_sem.at[2]),
        pltpu.make_async_copy(filt.at[pl.ds(me * width, width)], land_filt.at[me], local_sem.at[3]),
        pltpu.make_async_copy(gate.at[pl.ds(me * width, width)], land_gate.at[me], local_sem.at[4]),
        pltpu.make_async_copy(
            upstream.at[pl.ds(me * rows, half)], owned.at[0:half, my_cols], local_sem.at[5]
        ),
        pltpu.make_async_copy(
            upstream.at[pl.ds(me * rows + half + mz * part, part)],
            owned.at[part_rows, my_cols],
            local_sem.at[6],
        ),
    ]
    for copy in local:
        copy.start()

    barrier = pltpu.get_barrier_semaphore()
    for r in range(1, n):
        pl.semaphore_signal(
            barrier,
            inc=1,
            device_id={"seq": (me + r) % n},
            device_id_type=pl.DeviceIdType.MESH,
        )
    for r in range(1, nz):
        pl.semaphore_signal(
            barrier,
            inc=1,
            device_id={"chan": (mz + r) % nz},
            device_id_type=pl.DeviceIdType.MESH,
        )
    pl.semaphore_wait(barrier, n + nz - 2)

    sends = []

    def spread(source, land, send, recv):
        for r in range(1, n):
            peer = (me + r) % n
            copy = remote(
                source.at[pl.ds(peer * width, width)], land.at[me], send.at[r], recv.at[me], peer
            )
            copy.start()
            sends.append(copy)

    spread(hidden, land_hidden, hid_send, hid_recv)
    local[0].wait()

    def add_square(i, acc):
        part = hidden_own[pl.ds(pl.multiple_of(i * 32, 32), 32), :].astype(F32)
        part = part * part
        return acc + (part[0:8] + part[8:16]) + (part[16:24] + part[24:32])

    sq_land[mz] = lax.fori_loop(0, wide // 32, add_square, jnp.zeros((8, cols), F32), unroll=4)
    for r in range(1, nz):
        peer = (mz + r) % nz
        copy = remote(
            sq_land.at[mz], sq_land.at[mz], sq_send.at[r], sq_recv.at[mz], peer, "chan"
        )
        copy.start()
        sends.append(copy)
    for r in range(1, nz):
        peer = (mz + r) % nz
        remote(
            sq_land.at[mz], sq_land.at[peer], sq_send.at[r], sq_recv.at[peer], peer, "chan"
        ).wait_recv()
    squares = sq_land[0]
    for z in range(1, nz):
        squares = squares + sq_land[z]
    squares = jnp.sum(squares, axis=0, keepdims=True)
    inverse = lax.rsqrt(squares / total + EPSILON)
    inv_land[me] = jnp.broadcast_to(inverse, (8, cols))
    for r in range(1, n):
        peer = (me + r) % n
        copy = remote(inv_land.at[me], inv_land.at[me], inv_send.at[r], inv_recv.at[me], peer)
        copy.start()
        sends.append(copy)

    spread(filt, land_filt, fil_send, fil_recv)
    spread(gate, land_gate, gat_send, gat_recv)
    for r in range(1, n):
        peer = (me + r) % n
        copy = remote(
            upstream.at[pl.ds(peer * rows + half + mz * part, part)],
            owned.at[part_rows, my_cols],
            part_send.at[r],
            part_recv.at[me],
            peer,
        )
        copy.start()
        sends.append(copy)
    for r in range(1, n):
        peer = (me + r) % n
        copy = remote(
            upstream.at[pl.ds(peer * rows, half)],
            owned.at[0:half, my_cols],
            up_send.at[r],
            up_recv.at[me],
            peer,
        )
        copy.start()
        sends.append(copy)

    def arrived(land, send, recv):
        for r in range(1, n):
            peer = (me + r) % n
            remote(land.at[me], land.at[peer], send.at[r], recv.at[peer], peer).wait_recv()

    local[1].wait()
    local[2].wait()
    local[3].wait()
    local[4].wait()
    arrived(land_hidden, hid_send, hid_recv)
    arrived(inv_land, inv_send, inv_recv)
    for p in range(n):
        for k in range(per):
            lanes = slice(k * block, (k + 1) * block)
            spot = slice((p * per + k) * width, (p * per + k + 1) * width)
            xs[spot, :] = land_hidden[p, :, lanes].astype(F32) * inv_land[p, 0:1, lanes]
    arrived(land_filt, fil_send, fil_recv)
    for p in range(n):
        for k in range(per):
            lanes = slice(k * block, (k + 1) * block)
            spot = slice((p * per + k) * width, (p * per + k + 1) * width)
            hs[spot, :] = land_filt[p, :, lanes].astype(F32)
    arrived(land_gate, gat_send, gat_recv)
    for p in range(n):
        for k in range(per):
            lanes = slice(k * block, (k + 1) * block)
            spot = slice((p * per + k) * width, (p * per + k + 1) * width)
            gs[spot, :] = land_gate[p, :, lanes].astype(F32)

    lane_at = lax.broadcasted_iota(jnp.int32, (block, block), 1)
    row_at = lax.broadcasted_iota(jnp.int32, (block, block), 0)
    causal = lane_at >= row_at
    block_at = lax.broadcasted_iota(jnp.int32, (blocks, block), 0)

    def circulant(row):
        return pltpu.roll(
            jnp.broadcast_to(row, (block, block)), 0, 1, stride=1, stride_axis=0
        )

    def later(value, by):
        if by == 0:
            return value
        return jnp.where(block_at >= by, pltpu.roll(value, by, 0), 0.0)

    def channel(c, carry):
        mine = pl.ds(c, blocks, stride=width)
        x = (xs[mine, :] * gain[me * width + c]).astype(BF16)
        turned = circulant(taps_own[pl.ds(c, 1), :])
        now = jnp.where(causal, turned, 0.0).astype(BF16)
        before = jnp.where(causal, 0.0, turned).astype(BF16)
        pair = jnp.concatenate([x, later(x.astype(F32), 1).astype(BF16)], axis=1)
        short = jnp.dot(
            pair, jnp.concatenate([now, before], axis=0), preferred_element_type=F32
        )
        short = short.astype(BF16).astype(F32)
        acc = bias[me * width + c] * short
        held = jnp.zeros((block, block), F32)
        step = 2 if blocks % 2 == 0 else 1
        for d in range(0, blocks, step):
            signal, table = [], []
            for e in range(d, d + step):
                turned = circulant(hs[pl.ds(e * width + c, 1), :])
                table.append(jnp.where(causal, turned, held).astype(BF16))
                held = turned
                signal.append(later(short, e).astype(BF16))
            acc = acc + jnp.dot(
                jnp.concatenate(signal, axis=1),
                jnp.concatenate(table, axis=0),
                preferred_element_type=F32,
            )
        ms[mine, :] = gs[mine, :] * acc.astype(BF16).astype(F32)
        return carry

    other = me + 1 - 2 * (me % 2)

    def piece(src, g):
        return whole.at[src, pl.ds(g * share, share)]

    def forward(g):
        for k in range(1, n // 2):
            source = (me + 2 * k) % n
            remote(
                piece(me, g), piece(source, g), mix_send.at[g, k], mix_recv.at[g, source], source
            ).wait_recv()
            copy = remote(
                piece(source, g),
                piece(source, g),
                fwd_send.at[g, k],
                mix_recv.at[g, source],
                other,
            )
            copy.start()
            sends.append(copy)

    def share_part():
        local[6].wait()
        for r in range(1, n):
            peer = (me + r) % n
            remote(
                upstream.at[pl.ds(0, part)],
                owned.at[part_rows, pl.ds(pl.multiple_of(peer * cols, 128), cols)],
                part_send.at[r],
                part_recv.at[peer],
                peer,
            ).wait_recv()
        for r in range(1, nz):
            peer = (mz + r) % nz
            copy = remote(
                owned.at[part_rows],
                owned.at[part_rows],
                plane_send.at[r],
                plane_recv.at[mz],
                peer,
                "chan",
            )
            copy.start()
            sends.append(copy)

    for g in range(groups):
        lax.fori_loop(g * share, (g + 1) * share, channel, 0, unroll=8)
        for b in range(blocks):
            start = b * width + g * share
            whole[me, g * share : (g + 1) * share, b * block : (b + 1) * block] = ms[
                start : start + share, :
            ].astype(BF16)
        for k in range(1, n // 2):
            peer = (me + 2 * k) % n
            copy = remote(
                piece(me, g), piece(me, g), mix_send.at[g, k], mix_recv.at[g, me], peer
            )
            copy.start()
            sends.append(copy)
        copy = remote(piece(me, g), piece(me, g), mix_send.at[g, 0], mix_recv.at[g, me], other)
        copy.start()
        sends.append(copy)
        if g == min(1, groups - 1):
            share_part()
        if g > 0:
            forward(g - 1)
    forward(groups - 1)

    local[5].wait()
    for r in range(1, n):
        peer = (me + r) % n
        remote(
            upstream.at[pl.ds(0, half)],
            owned.at[0:half, pl.ds(pl.multiple_of(peer * cols, 128), cols)],
            up_send.at[r],
            up_recv.at[peer],
            peer,
        ).wait_recv()

    for r in range(1, nz):
        peer = (mz + r) % nz
        remote(
            owned.at[part_rows],
            owned.at[pl.ds(pl.multiple_of(half + peer * part, 16), part)],
            plane_send.at[r],
            plane_recv.at[peer],
            peer,
            "chan",
        ).wait_recv()

    for k in range(n // 2):
        source = (other + 2 * k) % n
        for g in range(groups):
            remote(
                piece(me, g), piece(source, g), mix_send.at[g, 0], mix_recv.at[g, source], other
            ).wait_recv()

    for p in range(n):
        out_mixed[p * width : (p + 1) * width, :] = whole[p, :, my_cols]

    sources = max(2, 128 // width)
    tile = min(rows, 128)
    for q in range(n // sources):
        right = whole[q * sources : (q + 1) * sources].reshape(sources * width, seq_len)

        def multiply(i, carry):
            at = pl.ds(pl.multiple_of(i * tile, tile), tile)
            out_grad[at, q * sources * width : (q + 1) * sources * width] = lax.dot_general(
                owned[at, :], right, (((1,), (1,)), ((), ())), preferred_element_type=F32
            )
            return carry

        lax.fori_loop(0, rows // tile, multiply, 0)

    for copy in sends:
        copy.wait_send()


def shards(hidden_states, norm_gain, short_filter, long_filter, long_bias, gate_stream, upstream):
    n = lax.axis_size("seq")
    nz = lax.axis_size("chan")
    wide, cols = hidden_states.shape
    width = wide // n
    rows = upstream.shape[0] // n
    seq_len = cols * n
    groups = max(1, width // 32)
    block = short_filter.shape[1]
    anywhere = pl.BlockSpec(memory_space=pl.ANY)
    scalars = pl.BlockSpec(memory_space=pltpu.SMEM)
    vmem = pl.BlockSpec(memory_space=pltpu.VMEM)
    dma = pltpu.SemaphoreType.DMA
    flat = (seq_len // block * width, block)
    return pl.pallas_call(
        functools.partial(body, n, nz, groups),
        out_shape=(
            jax.ShapeDtypeStruct((wide, cols), BF16),
            jax.ShapeDtypeStruct((rows, wide), F32),
        ),
        in_specs=[anywhere, scalars, anywhere, anywhere, scalars, anywhere, anywhere],
        out_specs=(vmem, vmem),
        scratch_shapes=[
            pltpu.VMEM((wide, cols), BF16),
            pltpu.VMEM((n, width, cols), BF16),
            pltpu.VMEM((n, width, cols), BF16),
            pltpu.VMEM((n, width, cols), BF16),
            pltpu.VMEM((width, block), F32),
            pltpu.VMEM((nz, 8, cols), F32),
            pltpu.VMEM((n, 8, cols), F32),
            pltpu.VMEM((rows, seq_len), BF16),
            pltpu.VMEM((n, width, seq_len), BF16),
            pltpu.VMEM(flat, F32),
            pltpu.VMEM(flat, F32),
            pltpu.VMEM(flat, F32),
            pltpu.VMEM(flat, F32),
            dma((7,)),
            dma((n,)),
            dma((n,)),
            dma((n,)),
            dma((n,)),
            dma((n,)),
            dma((n,)),
            dma((n,)),
            dma((n,)),
            dma((n,)),
            dma((n,)),
            dma((nz,)),
            dma((nz,)),
            dma((nz,)),
            dma((nz,)),
            dma((n,)),
            dma((n,)),
            dma((groups, n)),
            dma((groups, n)),
            dma((groups, n)),
        ],
        compiler_params=pltpu.CompilerParams(
            collective_id=0, has_side_effects=True, vmem_limit_bytes=48 * 1024 * 1024
        ),
        name="hyena",
    )(hidden_states, norm_gain, short_filter, long_filter, long_bias, gate_stream, upstream)


def solution(mesh):
    placed = (
        P("chan", "seq"),
        P("chan"),
        P("chan", None),
        P("chan", "seq"),
        P("chan"),
        P("chan", "seq"),
        P(None, "seq"),
    )
    return jax.shard_map(
        shards,
        mesh=mesh,
        in_specs=placed,
        out_specs=(P("chan", "seq"), P("seq", "chan")),
        check_vma=False,
    )
```
